32 devices in a mesh: dp: 16 (over z, x, core), mp: 2 (over y).
Axes of the slice: x: 2, y: 2, z: 4, core: 2. Of those that a mesh axis runs over, the one named last changes fastest.
Arguments:
- tokens: bfloat16 [512, 16384], P('dp', 'mp'), may hold values from -6 to 6
- gate_weight: bfloat16 [16384, 28672], P('mp', 'dp'), may hold values from -0.046875 to 0.046875
- up_weight: bfloat16 [16384, 28672], P('mp', 'dp'), may hold values from -0.046875 to 0.046875
- down_weight: bfloat16 [28672, 16384], P('dp', 'mp'), may hold values from -0.03125 to 0.03125
Outputs:
- mixed: bfloat16 [512, 16384], P('dp', 'mp')
The draws below stay inside these ranges and needn't reach their ends.
All inputs are finite; a program needn't handle non-finite values.
Results may differ from the reference program's by a relative error of at most 0.0049.
Values may be sent and summed in bfloat16 or wider, within the bound.
No kernel may reach another device: no remote copies, remote signals or barrier semaphores. Data moves between devices by JAX's collectives and lax.ppermute only.
A program may use at most 192 MiB of HBM per device.

```python
import jax
import jax.numpy as jnp

D = 16384
FF = 28672
TOKENS = 512


def block_scale(own_key, dims, pieces, low, largest):
    def one(position, blocks):
        heights = jax.random.uniform(jax.random.fold_in(jax.random.fold_in(own_key, 6), position), (blocks,), jnp.float32, low / len(pieces), largest / len(pieces))
        return jnp.repeat(jnp.exp(heights), dims[position] // blocks).reshape((-1,) + (1,) * (len(dims) - position - 1))

    gain = one(*pieces[0])
    for cut in pieces[1:]:
        gain = gain * one(*cut)
    return gain


def noise(own_key, shape, width, most, cuts=(), held_as=jnp.bfloat16):
    drawn = jax.random.normal(own_key, shape, jnp.float32) * width
    if len(cuts) > 0:
        drawn = block_scale(own_key, shape, cuts, -0.22, 0.18) * drawn
    return jnp.clip(drawn, min=-most, max=most).astype(held_as)


def setup_inputs(seed: int = 0) -> dict:
    splits = jax.random.split(jax.random.key(seed), 5)
    tokens = noise(splits[0], (TOKENS, D), 1.0, 6.0, ((0, 16), (1, 2)))
    gate_weight = noise(splits[1], (D, FF), D ** -0.5, 0.046875, ((0, 2), (1, 16)))
    up_weight = noise(splits[2], (D, FF), D ** -0.5, 0.046875, ((0, 2), (1, 16)))
    down_weight = noise(splits[3], (FF, D), FF ** -0.5, 0.03125, ((0, 16), (1, 2)))
    return dict(tokens=tokens, gate_weight=gate_weight, up_weight=up_weight, down_weight=down_weight)


def reference(tokens, gate_weight, up_weight, down_weight):
    gate = jnp.dot(tokens, gate_weight, preferred_element_type=jnp.float32)
    up = jnp.dot(tokens, up_weight, preferred_element_type=jnp.float32)
    hidden = (jax.nn.silu(gate) * up).astype(jnp.bfloat16)
    return jnp.dot(hidden, down_weight, preferred_element_type=jnp.float32).astype(jnp.bfloat16)
```

```python
import functools

import jax
import jax.numpy as jnp
from jax import lax
from jax.experimental import pallas as pl
from jax.experimental.pallas import tpu as pltpu
from jax.sharding import PartitionSpec as P

ANY = pl.BlockSpec(memory_space=pl.ANY)


def swap(value, axis, size, mask):
    return lax.ppermute(value, axis, [(i, i ^ mask) for i in range(size)])


def tile_of(width, most):
    tile = most
    while width % tile:
        tile -= 128
    return tile


def load_parts(parts, place, held, sems):
    copies = [
        pltpu.make_async_copy(part, held.at[place(i, part)], sems.at[i])
        for i, part in enumerate(parts)
    ]
    for copy in copies:
        copy.start()
    for copy in copies:
        copy.wait()


def expand_kernel(groups, *refs):
    pieces = len(refs) - groups - 4
    parts, (gate_w, up_w), outs, (held, sems) = (
        refs[:pieces],
        refs[pieces : pieces + 2],
        refs[pieces + 2 : -2],
        refs[-2:],
    )
    each = pieces // groups
    rows = parts[0].shape[0]
    me = lax.axis_index("mp")

    @pl.when(pl.program_id(0) == 0)
    def _():
        def place(i, part):
            group = jnp.bitwise_xor(me, i // each)
            start = group * (each * rows) + (i % each) * rows
            return pl.ds(pl.multiple_of(start, rows), rows), slice(None)

        load_parts(parts, place, held, sems)

    kept = each * rows
    for which, weight in enumerate((gate_w, up_w)):
        total = jnp.dot(held[...], weight[...], preferred_element_type=jnp.float32)
        for k, out in enumerate(outs):
            out[which] = total[k * kept : (k + 1) * kept].astype(out.dtype)


def expand(pieces, gate_weight, up_weight, groups, first, count, tile):
    rows, depth = pieces[0].shape
    total = rows * len(pieces)
    kept = total // groups
    width = count * tile
    weight_spec = pl.BlockSpec((depth, tile), lambda j: (0, j + first))
    out_spec = pl.BlockSpec((2, kept, tile), lambda j: (0, 0, j))
    return pl.pallas_call(
        functools.partial(expand_kernel, groups),
        grid=(count,),
        in_specs=[ANY] * len(pieces) + [weight_spec] * 2,
        out_specs=[out_spec] * groups,
        out_shape=[
            jax.ShapeDtypeStruct((2, kept, width), jnp.bfloat16 if k else jnp.float32)
            for k in range(groups)
        ],
        scratch_shapes=[
            pltpu.VMEM((total, depth), jnp.bfloat16),
            pltpu.SemaphoreType.DMA((len(pieces),)),
        ],
        compiler_params=pltpu.CompilerParams(vmem_limit_bytes=48 * 2**20),
        cost_estimate=pl.CostEstimate(
            flops=4 * total * depth * width,
            bytes_accessed=4 * depth * width + 2 * total * depth + 8 * total * width,
            transcendentals=0,
        ),
        name="expand",
    )(*pieces, gate_weight, up_weight)


def contract_kernel(groups, spans, *refs):
    parts, weight, (kept, sent), (held, sems) = refs[:-5], refs[-5], refs[-4:-2], refs[-2:]
    rows = parts[0].shape[0]
    me = lax.axis_index("mp")

    @pl.when(pl.program_id(0) == 0)
    def _():
        def place(i, part):
            group = jnp.bitwise_xor(me, i // len(spans))
            start, size = spans[i % len(spans)]
            return pl.ds(pl.multiple_of(group * rows, rows), rows), pl.ds(start, size)

        load_parts(parts, place, held, sems)

    total = jnp.dot(held[...], weight[...], preferred_element_type=jnp.float32)
    half = total.shape[0] // 2
    kept[...] = total[:half]
    sent[...] = total[half:].astype(sent.dtype)


def contract(hidden, down_weight, first, count, tile):
    groups = len(hidden)
    depth = down_weight.shape[0]
    spans, start = [], 0
    for part in hidden[0]:
        spans.append((start, part.shape[1]))
        start += part.shape[1]
    parts = [part for group in hidden for part in group]
    total = parts[0].shape[0] * groups
    width = count * tile
    out_spec = pl.BlockSpec((total // 2, tile), lambda j: (0, j))
    return pl.pallas_call(
        functools.partial(contract_kernel, groups, tuple(spans)),
        grid=(count,),
        in_specs=[ANY] * len(parts) + [pl.BlockSpec((depth, tile), lambda j: (0, j + first))],
        out_specs=[out_spec] * 2,
        out_shape=[
            jax.ShapeDtypeStruct((total // 2, width), jnp.float32),
            jax.ShapeDtypeStruct((total // 2, width), jnp.bfloat16),
        ],
        scratch_shapes=[
            pltpu.VMEM((total, depth), jnp.bfloat16),
            pltpu.SemaphoreType.DMA((len(parts),)),
        ],
        compiler_params=pltpu.CompilerParams(vmem_limit_bytes=48 * 2**20),
        cost_estimate=pl.CostEstimate(
            flops=2 * total * depth * width,
            bytes_accessed=2 * depth * width + 2 * total * depth + 6 * total * width // 2,
            transcendentals=0,
        ),
        name="contract",
    )(*parts, down_weight)


def cuts(count, pieces):
    edges = [count * i // pieces for i in range(pieces + 1)]
    return [(a, b - a) for a, b in zip(edges, edges[1:]) if b > a]


def per_device(n_dp, n_mp, tokens, gate_weight, up_weight, down_weight):
    n_z = n_dp // 4
    rows = tokens.shape[0]
    f32, bf16 = jnp.float32, jnp.bfloat16
    dp = lambda value, mask: swap(value, "dp", n_dp, mask)
    mp = lambda value, mask: swap(value, "mp", n_mp, mask)
    chunks = [list(range(0, n_z, 2)), list(range(1, n_z, 2))]
    order = chunks[0] + chunks[1]

    far = {d: tokens if d == 0 else dp(tokens, 4 * d) for d in order}
    across = {d: dp(far[d], 2) for d in order}
    other = {(x, d): dp(v[d], 1) for d in order for x, v in enumerate((far, across))}

    width = gate_weight.shape[1]
    tile = tile_of(width, 256)
    features = down_weight.shape[1]
    tile_down = tile_of(features, 1024)
    finals = {}
    for index, chunk in enumerate(chunks):
        pieces = [far[d] for d in chunk] + [across[d] for d in chunk]
        pieces += [other[x, d] for x in (0, 1) for d in chunk]
        hidden = [[] for _ in range(n_mp)]
        for first, count in cuts(width // tile, 2):
            own, *sends = expand(pieces, gate_weight, up_weight, n_mp, first, count, tile)
            both = own
            for k, send in enumerate(sends, 1):
                both = both + mp(send, k).astype(f32)
            mine = (jax.nn.silu(both[0]) * both[1]).astype(bf16)
            hidden[0].append(mine)
            for k in range(1, n_mp):
                hidden[k].append(mp(mine, k))
        half = len(chunk) * rows
        for s, (first, count) in enumerate(cuts(features // tile_down, 2)):
            kept, sent = contract(hidden, down_weight, first, count, tile_down)
            core = dp(sent, 1)
            met = dp((kept[half:] + core[half:].astype(f32)).astype(bf16), 2)
            column = kept[:half] + core[:half].astype(f32) + met.astype(f32)
            for i, d in enumerate(chunk):
                part = column[i * rows : (i + 1) * rows]
                finals[s, d] = part if d == 0 else dp(part.astype(bf16), 4 * d).astype(f32)
    out = []
    for s in sorted({s for s, _ in finals}):
        total = finals[s, 0]
        for d in order[1:]:
            total = total + finals[s, d]
        out.append(total.astype(bf16))
    return jnp.concatenate(out, axis=1)


def solution(mesh):
    return jax.shard_map(
        functools.partial(per_device, mesh.shape["dp"], mesh.shape["mp"]),
        mesh=mesh,
        in_specs=(P("dp", "mp"), P("mp", "dp"), P("mp", "dp"), P("dp", "mp")),
        out_specs=P("dp", "mp"),
        check_vma=False,
    )
```
